128 devices in a mesh: sample: 4 (over x_lo, core), freq: 32 (over y, z, x_hi).
Axes of the slice: x: 4 (x_hi: 2, x_lo: 2; x = x_hi * 2 + x_lo), y: 4, z: 4, core: 2. Of those that a mesh axis runs over, the one named last changes fastest.
Arguments:
- images: bfloat16 [1024, 32, 32, 128], P(('sample', 'freq')), may hold values from -6 to 6
- cotangent: bfloat16 [1024, 32, 32, 128], P(('sample', 'freq')), may hold values from -6 to 6
- kernel: float32 [3, 3, 128, 128], replicated, may hold values from -0.022097087 to 0.022097087
Outputs:
- outputs: bfloat16 [1024, 32, 32, 128], P(('sample', 'freq'))
- kernel_grad: float32 [3, 3, 128, 128], replicated
The draws below stay inside these ranges and needn't reach their ends.
All inputs are finite; a program needn't handle non-finite values.
Results may differ from the reference program's by a relative error of at most 0.0064.
Values may be sent and summed in bfloat16 or wider, within the bound.
A program may use at most 128 MiB of HBM per device.

```python
import math
import jax
import jax.numpy as jnp
from jax import lax

C = 128
SIDE = 32
TAPS = 3
NS_STEPS = 2
IMG_DEV = 8
HALF = 17
IMAGES = 1024


def draw_kernel(key, part):
    bound_value = 0.1 * 3.0 ** 0.5 / C ** 0.5
    return jax.random.uniform(key, (TAPS, TAPS, C, C), jnp.float32, -bound_value, bound_value)


def block_levels(stream_key, dims, cuts, low, high):
    loudness, own = 1.0, jax.random.fold_in(stream_key, 6)
    for dim, blocks in cuts:
        draws = jnp.exp(jax.random.uniform(jax.random.fold_in(own, dim), (blocks,), jnp.float32, low / len(cuts), high / len(cuts)))
        loudness = loudness * jnp.repeat(draws, dims[dim] // blocks).reshape([-1 if axis == dim else 1 for axis in range(len(dims))])
    return loudness


def centred(own_key, shape, scale, limit, cuts=(), kind=jnp.bfloat16):
    values = scale * jax.random.normal(own_key, shape, jnp.float32)
    if cuts:
        values = values * block_levels(own_key, shape, cuts, -0.22, 0.18)
    return jnp.clip(values, -limit, limit).astype(kind)


def setup_inputs(seed: int = 0) -> dict:
    splits = jax.random.split(jax.random.key(seed), 4)
    return {
        "images": centred(splits[0], (IMAGES, SIDE, SIDE, C), 1.0, 6.0, ((0, 128),)),
        "cotangent": centred(splits[1], (IMAGES, SIDE, SIDE, C), 1.0, 6.0, ((0, 128),)),
        "kernel": draw_kernel(jax.random.fold_in(splits[3], 71), 0),
    }


HIGHEST = lax.Precision.HIGHEST


def angle_tables(side_cells, half_cells):
    position = jnp.arange(side_cells, dtype=jnp.int32)
    columns = jnp.arange(half_cells, dtype=jnp.int32)
    across = (position[:, None] * columns[None, :]) % side_cells
    square = (position[:, None] * position[None, :]) % side_cells
    radians = 2.0 * math.pi / side_cells
    return radians * across.astype(jnp.float32), radians * square.astype(jnp.float32)


def forward_spectrum(pictures, across_angle, square_angle):
    number = pictures.shape[0]
    side_cells = pictures.shape[1]
    channels = pictures.shape[3]
    half_cells = across_angle.shape[1]
    row_table = jnp.concatenate([jnp.cos(across_angle), -jnp.sin(across_angle)], axis=1)
    partial_sum = jnp.einsum("nhwc,wk->nhkc", pictures.astype(jnp.float32), row_table, precision=HIGHEST)
    partial_sum = partial_sum.reshape(number, side_cells, 2, half_cells, channels)
    cosine = jnp.cos(square_angle)
    sine_table = jnp.sin(square_angle)
    rotation = jnp.stack([jnp.stack([cosine, sine_table]), jnp.stack([-sine_table, cosine])])
    spectrum = jnp.einsum("abuh,nhbvc->nuvac", rotation, partial_sum, precision=HIGHEST)
    return spectrum.reshape(number, side_cells, half_cells, 2 * channels).astype(jnp.bfloat16)


def inverse_spectrum(spectrum, across_angle, square_angle):
    number = spectrum.shape[0]
    side_cells = spectrum.shape[1]
    half_cells = spectrum.shape[2]
    channels = spectrum.shape[3] // 2
    pieces = spectrum.astype(jnp.float32).reshape(number, side_cells, half_cells, 2, channels)
    cosine = jnp.cos(square_angle)
    sine_table = jnp.sin(square_angle)
    rotation = jnp.stack([jnp.stack([cosine, -sine_table]), jnp.stack([sine_table, cosine])])
    column_sum = jnp.einsum("abuh,nuvbc->nhavc", rotation, pieces, precision=HIGHEST)
    frequency = jnp.arange(half_cells, dtype=jnp.int32)
    boundary = (frequency == 0) | (frequency == side_cells // 2)
    weights = jnp.where(boundary, 1.0, 2.0).astype(jnp.float32) / (side_cells * side_cells)
    back_table = jnp.concatenate([jnp.cos(across_angle).T * weights[:, None], -jnp.sin(across_angle).T * weights[:, None]], axis=0)
    result = jnp.einsum("nhkc,kw->nhwc", column_sum.reshape(number, side_cells, 2 * half_cells, channels), back_table, precision=HIGHEST)
    return result.astype(jnp.bfloat16)


def tap_angles(row_numbers, side_cells, half_cells, tap_count):
    offsets = jnp.arange(tap_count, dtype=jnp.int32) - (tap_count - 1) // 2
    columns = jnp.arange(half_cells, dtype=jnp.int32)
    phases = (row_numbers[:, None, None, None] * offsets[None, None, :, None] + columns[None, :, None, None] * offsets[None, None, None, :]) % side_cells
    phases = phases.reshape(row_numbers.shape[0] * half_cells, tap_count * tap_count)
    return (2.0 * math.pi / side_cells) * phases.astype(jnp.float32)


def skew_matrix(kernel, angles):
    flattened = kernel.reshape(kernel.shape[0] * kernel.shape[1], kernel.shape[2], kernel.shape[3])
    real_part = jnp.einsum("ft,toi->foi", jnp.cos(angles), flattened, precision=HIGHEST)
    imag_part = -jnp.einsum("ft,toi->foi", jnp.sin(angles), flattened, precision=HIGHEST)
    return (real_part - jnp.swapaxes(real_part, 1, 2), imag_part + jnp.swapaxes(imag_part, 1, 2))


def rounded(matrix):
    return lax.optimization_barrier(matrix.astype(jnp.bfloat16)).astype(jnp.float32)


def low_multiply(former, latter):
    return jnp.einsum("fij,fjk->fik", rounded(former), rounded(latter))


def full_multiply(former, latter):
    return jnp.einsum("fij,fjk->fik", former, latter, precision=HIGHEST)


def complex_product(former, latter, multiply):
    real_out = multiply(former[0], latter[0]) - multiply(former[1], latter[1])
    imag_out = multiply(former[0], latter[1]) + multiply(former[1], latter[0])
    return (real_out, imag_out)


def adjoint(matrix):
    return (jnp.swapaxes(matrix[0], 1, 2), -jnp.swapaxes(matrix[1], 1, 2))


def cayley_deviation(skew_part):
    deviation = (-skew_part[0], -skew_part[1])
    for iteration in range(NS_STEPS):
        cross_term = complex_product(skew_part, deviation, low_multiply)
        residue = (-(skew_part[0] + deviation[0] + cross_term[0]), -(skew_part[1] + deviation[1] + cross_term[1]))
        update = complex_product(deviation, residue, low_multiply)
        deviation = (deviation[0] + residue[0] + update[0], deviation[1] + residue[1] + update[1])
    return deviation


def embedded(deviation):
    doubled_real = (2.0 * deviation[0]).astype(jnp.bfloat16)
    doubled_imag = (2.0 * deviation[1]).astype(jnp.bfloat16)
    upper_half = jnp.concatenate([doubled_real, -doubled_imag], axis=2)
    lower_half = jnp.concatenate([doubled_imag, doubled_real], axis=2)
    return jnp.concatenate([upper_half, lower_half], axis=1)


def grad_factor(side_cells, half_cells, total_images):
    frequency = jnp.arange(half_cells, dtype=jnp.int32)
    boundary = (frequency == 0) | (frequency == side_cells // 2)
    return jnp.where(boundary, 2.0, 4.0).astype(jnp.float32) / (side_cells * side_cells * total_images)


def skew_gradient(spec_grad, deviation):
    conjugate = adjoint(deviation)
    partial_term = complex_product(spec_grad, conjugate, full_multiply)
    partial_term = (spec_grad[0] + partial_term[0], spec_grad[1] + partial_term[1])
    outer_term = complex_product(conjugate, partial_term, full_multiply)
    return (-(partial_term[0] + outer_term[0]), -(partial_term[1] + outer_term[1]))


def kernel_piece(skew_grad, angles, tap_count):
    sym_real = skew_grad[0] - jnp.swapaxes(skew_grad[0], 1, 2)
    sym_imag = skew_grad[1] + jnp.swapaxes(skew_grad[1], 1, 2)
    piece_sum = jnp.einsum("ft,foi->toi", jnp.cos(angles), sym_real, precision=HIGHEST) - jnp.einsum("ft,foi->toi", jnp.sin(angles), sym_imag, precision=HIGHEST)
    return piece_sum.reshape(tap_count, tap_count, sym_real.shape[1], sym_real.shape[2])


def reference(images, cotangent, kernel):
    across_angle, square_angle = angle_tables(SIDE, HALF)
    block_count = IMAGES // IMG_DEV

    def forward_block(pictures):
        return forward_spectrum(pictures, across_angle, square_angle)

    image_spectrum = lax.map(forward_block, images.reshape(block_count, IMG_DEV, SIDE, SIDE, C)).reshape(IMAGES, SIDE, HALF, 2 * C)
    tangent_spectrum = lax.map(forward_block, cotangent.reshape(block_count, IMG_DEV, SIDE, SIDE, C)).reshape(IMAGES, SIDE, HALF, 2 * C)
    factor = grad_factor(SIDE, HALF, IMAGES)

    def row_work(row_index):
        image_row = lax.dynamic_index_in_dim(image_spectrum, row_index, 1, keepdims=False)
        tangent_row = lax.dynamic_index_in_dim(tangent_spectrum, row_index, 1, keepdims=False)
        angles = tap_angles(jnp.reshape(row_index, (1,)).astype(jnp.int32), SIDE, HALF, TAPS)
        skew_part = skew_matrix(kernel, angles)
        deviation = cayley_deviation(skew_part)
        operator = embedded(deviation)
        image_float = image_row.astype(jnp.float32)
        answer_row = (image_float + jnp.einsum("nfj,fkj->nfk", image_float, operator.astype(jnp.float32))).astype(jnp.bfloat16)
        outer_sum = jnp.einsum("nfk,nfj->fkj", tangent_row.astype(jnp.float32), image_float)
        grad_real = (outer_sum[:, :C, :C] + outer_sum[:, C:, C:]) * factor[:, None, None]
        grad_imag = (outer_sum[:, C:, :C] - outer_sum[:, :C, C:]) * factor[:, None, None]
        skew_grad = skew_gradient((grad_real, grad_imag), deviation)
        return answer_row, kernel_piece(skew_grad, angles, TAPS)

    answer_rows, kernel_parts = lax.map(row_work, jnp.arange(SIDE, dtype=jnp.int32))
    answer_spectrum = jnp.transpose(answer_rows, (1, 0, 2, 3))

    def inverse_block(spectrum):
        return inverse_spectrum(spectrum, across_angle, square_angle)

    outputs = lax.map(inverse_block, answer_spectrum.reshape(block_count, IMG_DEV, SIDE, HALF, 2 * C)).reshape(IMAGES, SIDE, SIDE, C)
    kernel_grad = jnp.sum(kernel_parts, axis=0)
    return outputs, kernel_grad
```

```python
import functools
import math

import jax
import jax.numpy as jnp
import numpy as np
from jax import lax
from jax.experimental import pallas as pl
from jax.experimental.pallas import tpu as pltpu
from jax.sharding import PartitionSpec as P

NS_STEPS = 2


def transform_tables(side, images):
    half = side // 2
    freq = np.arange(half)
    cell = np.arange(side)
    angle = 2.0 * math.pi / side * ((freq[:, None] * cell[None, :]) % side)
    real_rows = np.cos(angle)
    imag_rows = -np.sin(angle)
    imag_rows[0] = np.where(cell % 2 == 0, 1.0, -1.0)
    forward = np.stack([real_rows, imag_rows])
    weight = np.full((2, half, 1), 2.0 / side)
    weight[:, 0] = 1.0 / side
    same = np.eye(images)
    analysis = np.einsum("asw,nm->asnmw", forward, same).reshape(side * images, images * side)
    synthesis = np.einsum("asw,nm->nwasm", forward * weight, same).reshape(images * side, side * images)
    return analysis, synthesis


def slot_tables(side, total_images):
    half = side // 2
    angle = 2.0 * math.pi / side * np.arange(half)
    cos_a, cos_b, sine = np.cos(angle), np.cos(angle), np.sin(angle)
    cos_b[0] = -1.0
    sine[0] = 0.0
    scale = np.full(half, -2.0 * 2.0 / (total_images * side))
    scale[0] *= 0.5
    return np.stack([cos_a, cos_b, sine, scale]).astype(np.float32)


def local_kernel(
    images, channels, side, group, slot_table, pictures_hbm, cotangent_hbm, taps_hbm, analysis_hbm, synthesis_hbm,
    outputs_hbm, pieces_ref,
    pictures, cotangent, taps, analysis, synthesis, mixes, weights, base, state, other, partner, answer, total,
    result, in_sem, out_sem,
):
    half = side // 2
    pair = 2 * images
    rows = side * pair
    wide = 2 * channels

    loads = [
        pltpu.make_async_copy(taps_hbm, taps, in_sem.at[0]),
        pltpu.make_async_copy(analysis_hbm, analysis, in_sem.at[1]),
        pltpu.make_async_copy(pictures_hbm, pictures, in_sem.at[2]),
        pltpu.make_async_copy(cotangent_hbm, cotangent, in_sem.at[3]),
        pltpu.make_async_copy(synthesis_hbm, synthesis, in_sem.at[4]),
    ]
    for load in loads:
        load.start()
    loads[0].wait()
    for row in range(3):
        across = [taps[row, col].T - taps[2 - row, 2 - col] for col in range(3)]
        mixes[row, 0] = across[1]
        mixes[row, 1] = across[2] + across[0]
        mixes[row, 2] = across[0] - across[2]
    total[...] = jnp.zeros_like(total)
    for load in loads[1:4]:
        load.wait()

    def analyse(h, carry):
        both = jnp.concatenate(
            [pictures[:, h].reshape(images * side, channels), cotangent[:, h].reshape(images * side, channels)], axis=1
        )
        spectrum = jnp.dot(analysis[...], both, preferred_element_type=jnp.float32)
        spectrum = spectrum.reshape(2, half, images, wide)
        spectrum = jnp.concatenate([spectrum[..., :channels], spectrum[..., channels:]], axis=2).astype(jnp.bfloat16)
        where = pl.ds(pl.multiple_of((h + 1) * pair, pair), pair)
        base[:, where, :channels] = spectrum[0]
        base[:, where, channels:] = spectrum[1]
        return carry

    lax.fori_loop(0, side, analyse, 0, unroll=4)
    base[:, :pair] = base[:, rows : rows + pair]
    base[:, rows + pair :] = base[:, pair : 2 * pair]

    def apply(source, weight):
        stacked = jnp.concatenate([source[2 * pair :], source[pair : rows + pair], source[:rows]], axis=1)
        return jnp.dot(stacked, weight, preferred_element_type=jnp.float32)

    def slot_group(index, carry):
        slots = [index * group + lane for lane in range(group)]
        for lane, slot in enumerate(slots):
            cos_a, cos_b, sine = slot_table[0, slot], slot_table[1, slot], slot_table[2, slot]
            for row in range(3):
                turned = (sine * mixes[row, 2]).astype(jnp.bfloat16)
                lo, hi = row * wide, row * wide + channels
                weights[lane, lo:hi, :channels] = (mixes[row, 0] + cos_a * mixes[row, 1]).astype(jnp.bfloat16)
                weights[lane, hi : hi + channels, channels:] = (mixes[row, 0] + cos_b * mixes[row, 1]).astype(jnp.bfloat16)
                weights[lane, lo:hi, channels:] = turned
                weights[lane, hi : hi + channels, :channels] = -turned
        powers = 2 ** (NS_STEPS + 1) - 1
        for step in range(powers):
            for lane, slot in enumerate(slots):
                source = base.at[slot] if step == 0 else (state if step % 2 else other).at[lane]
                target = (other if step % 2 else state).at[lane]
                product = apply(source, weights[lane]).reshape(side, 2, images, wide)
                start = base[slot, pair : rows + pair].astype(jnp.float32).reshape(side, 2, images, wide)
                forward = start[:, 0] - product[:, 0]
                backward = start[:, 1] + product[:, 1]
                joined = jnp.stack([forward, backward], axis=1).reshape(rows, wide).astype(jnp.bfloat16)
                target[pair : rows + pair] = joined
                if step < powers - 1:
                    target[:pair] = joined[rows - pair :]
                    target[rows + pair :] = joined[:pair]
                else:
                    answer[slot] = (2.0 * forward - start[:, 0]).reshape(side * images, wide)
                    crossed = jnp.stack([-backward, forward], axis=1).reshape(rows, wide).astype(jnp.bfloat16)
                    partner[lane, pair:] = crossed
                    partner[lane, :pair] = crossed[rows - pair :]
        last = state if powers % 2 else other
        for lane, slot in enumerate(slots):
            cos_a, cos_b, sine, scale = (slot_table[k, slot] for k in range(4))
            left = last[lane, pair : rows + pair]
            for row, right in enumerate((partner[lane, pair:], partner[lane, :rows])):
                outer = lax.dot_general(left, right, (((0,), (0,)), ((), ())), preferred_element_type=jnp.float32)
                outer = outer * scale
                first, second = outer[:channels, :channels], outer[channels:, channels:]
                total[row, 0] += first + second
                total[row, 1] += cos_a * first + cos_b * second
                total[row, 2] += sine * (outer[channels:, :channels] - outer[:channels, channels:])
        return carry

    lax.fori_loop(0, half // group, slot_group, 0)

    pieces_ref[0] = total[0, 0]
    pieces_ref[1] = total[0, 1] - total[0, 2]
    pieces_ref[2] = total[1, 0]
    pieces_ref[3] = total[1, 1] - total[1, 2]
    pieces_ref[4] = total[1, 1] + total[1, 2]
    loads[4].wait()

    def synthesise(index, carry):
        columns = []
        for part in range(2):
            where = pl.ds(pl.multiple_of((2 * index + part) * images, images), images)
            tiles = [answer[:, where, k * channels : (k + 1) * channels].reshape(half * images, channels) for k in range(2)]
            columns.append(jnp.concatenate(tiles, axis=0).astype(jnp.bfloat16))
        maps = jnp.dot(synthesis[...], jnp.concatenate(columns, axis=1), preferred_element_type=jnp.float32)
        maps = maps.astype(jnp.bfloat16)
        for part in range(2):
            result[:, 2 * index + part] = maps[:, part * channels : (part + 1) * channels].reshape(images, side, channels)
        return carry

    lax.fori_loop(0, side // 2, synthesise, 0, unroll=4)
    store = pltpu.make_async_copy(result, outputs_hbm, out_sem)
    store.start()
    store.wait()


def local_work(pictures, cotangent, kernel, total_images, group=2):
    images, side, _, channels = pictures.shape
    half = side // 2
    pair = 2 * images
    rows = side * pair
    wide = 2 * channels
    analysis, synthesis = transform_tables(side, images)
    analysis = jnp.asarray(analysis, jnp.bfloat16)
    synthesis = jnp.asarray(synthesis, jnp.bfloat16)
    table = jnp.asarray(slot_tables(side, total_images))
    anywhere = pl.BlockSpec(memory_space=pl.ANY)
    return pl.pallas_call(
        functools.partial(local_kernel, images, channels, side, group),
        out_shape=(
            jax.ShapeDtypeStruct(pictures.shape, jnp.bfloat16),
            jax.ShapeDtypeStruct((5, channels, channels), jnp.float32),
        ),
        in_specs=[pl.BlockSpec(memory_space=pltpu.SMEM)] + [anywhere] * 5,
        out_specs=(anywhere, pl.BlockSpec(memory_space=pltpu.VMEM)),
        scratch_shapes=[
            pltpu.VMEM(pictures.shape, jnp.bfloat16),
            pltpu.VMEM(pictures.shape, jnp.bfloat16),
            pltpu.VMEM(kernel.shape, jnp.float32),
            pltpu.VMEM((wide, wide), jnp.bfloat16),
            pltpu.VMEM((wide, wide), jnp.bfloat16),
            pltpu.VMEM((3, 3, channels, channels), jnp.float32),
            pltpu.VMEM((group, 3 * wide, wide), jnp.bfloat16),
            pltpu.VMEM((half, rows + 2 * pair, wide), jnp.bfloat16),
            pltpu.VMEM((group, rows + 2 * pair, wide), jnp.bfloat16),
            pltpu.VMEM((group, rows + 2 * pair, wide), jnp.bfloat16),
            pltpu.VMEM((group, rows + pair, wide), jnp.bfloat16),
            pltpu.VMEM((half, side * images, wide), jnp.float32),
            pltpu.VMEM((2, 3, channels, channels), jnp.float32),
            pltpu.VMEM(pictures.shape, jnp.bfloat16),
            pltpu.SemaphoreType.DMA((5,)),
            pltpu.SemaphoreType.DMA,
        ],
        compiler_params=pltpu.CompilerParams(vmem_limit_bytes=48 * 1024 * 1024),
        name="local_work",
    )(table, pictures, cotangent, kernel, analysis, synthesis)


def per_device(images, cotangent, kernel):
    total = images.shape[0] * lax.axis_size("sample") * lax.axis_size("freq")
    outputs, pieces = local_work(images, cotangent, kernel, total)
    pieces = lax.psum(pieces, ("sample", "freq"))
    flip = -jnp.swapaxes(pieces, 1, 2)
    kernel_grad = jnp.stack(
        [flip[3], flip[2], flip[4], flip[1], pieces[0], pieces[1], pieces[4], pieces[2], pieces[3]]
    )
    return outputs, kernel_grad.reshape(kernel.shape)


def solution(mesh):
    placed = P(("sample", "freq"), None, None, None)
    return jax.shard_map(
        per_device,
        mesh=mesh,
        in_specs=(placed, placed, P()),
        out_specs=(placed, P()),
        check_vma=False,
    )
```

```python
import functools
import math

import jax
import jax.numpy as jnp
import numpy as np
from jax import lax
from jax.experimental import pallas as pl
from jax.experimental.pallas import tpu as pltpu
from jax.sharding import PartitionSpec as P

NS_STEPS = 2
GAIN = 1.6245


def transform_tables(side, images):
    half = side // 2
    freq = np.arange(half)
    cell = np.arange(side)
    angle = 2.0 * math.pi / side * ((freq[:, None] * cell[None, :]) % side)
    real_rows = np.cos(angle)
    imag_rows = -np.sin(angle)
    imag_rows[0] = np.where(cell % 2 == 0, 1.0, -1.0)
    forward = np.stack([real_rows, imag_rows])
    weight = np.full((2, half, 1), 2.0 / side)
    weight[:, 0] = 1.0 / side
    same = np.eye(images)
    analysis = np.einsum("asw,nm->asnmw", forward, same).reshape(side * images, images * side)
    synthesis = np.einsum("asw,nm->nwasm", forward * weight, same).reshape(images * side, side * images)
    return GAIN * analysis, GAIN * synthesis


def slot_tables(side, total_images):
    half = side // 2
    angle = 2.0 * math.pi / side * np.arange(half)
    cos_a, cos_b, sine = np.cos(angle), np.cos(angle), np.sin(angle)
    cos_b[0] = -1.0
    sine[0] = 0.0
    scale = np.full(half, -2.0 * 2.0 / (total_images * side * GAIN**2))
    scale[0] *= 0.5
    return np.stack([cos_a, cos_b, sine, scale]).astype(np.float32)


def layer_kernel(
    images, channels, side, group, slot_table, pictures_hbm, cotangent_hbm, taps_hbm, analysis_hbm, synthesis_hbm,
    outputs_hbm, kernel_grad,
    pictures, cotangent, taps, analysis, synthesis, mixes, weights, base, state, other, partner, answer, total,
    result, chunks, from_partner, mine, received, gathered, in_sem, out_sem, core_sem, chip_send, chip_recv,
):
    half = side // 2
    pair = 2 * images
    rows = side * pair
    wide = 2 * channels
    sample, freq = lax.axis_index("sample"), lax.axis_index("freq")
    ring = lax.axis_size("freq")
    chips = lax.axis_size("sample") * ring // 2
    core = sample % 2
    chip = sample // 2 * ring + freq

    def place_of(to_chip, to_core):
        return (to_chip // ring * 2 + to_core, to_chip % ring)

    def remote(source, target, send, recv, to_chip, to_core):
        return pltpu.make_async_remote_copy(
            source, target, send, recv, device_id=place_of(to_chip, to_core), device_id_type=pl.DeviceIdType.MESH
        )

    barrier = pltpu.get_barrier_semaphore()

    def greet(ahead, carry):
        pl.semaphore_signal(
            barrier, inc=1, device_id=place_of((chip + ahead) % chips, core), device_id_type=pl.DeviceIdType.MESH
        )
        return carry

    lax.fori_loop(1, chips, greet, 0)
    pl.semaphore_signal(barrier, inc=1, device_id=place_of(chip, 1 - core), device_id_type=pl.DeviceIdType.MESH)

    loads = [
        pltpu.make_async_copy(taps_hbm, taps, in_sem.at[0]),
        pltpu.make_async_copy(analysis_hbm, analysis, in_sem.at[1]),
        pltpu.make_async_copy(pictures_hbm, pictures, in_sem.at[2]),
        pltpu.make_async_copy(cotangent_hbm, cotangent, in_sem.at[3]),
        pltpu.make_async_copy(synthesis_hbm, synthesis, in_sem.at[4]),
    ]
    for load in loads:
        load.start()
    loads[0].wait()
    for row in range(3):
        across = [taps[row, col].T - taps[2 - row, 2 - col] for col in range(3)]
        mixes[row, 0] = across[1]
        mixes[row, 1] = across[2] + across[0]
        mixes[row, 2] = across[0] - across[2]
    total[...] = jnp.zeros_like(total)
    for load in loads[1:4]:
        load.wait()

    def analyse(h, carry):
        both = jnp.concatenate(
            [pictures[:, h].reshape(images * side, channels), cotangent[:, h].reshape(images * side, channels)], axis=1
        )
        spectrum = jnp.dot(analysis[...], both, preferred_element_type=jnp.float32)
        spectrum = spectrum.reshape(2, half, images, wide)
        spectrum = jnp.concatenate([spectrum[..., :channels], spectrum[..., channels:]], axis=2).astype(jnp.bfloat16)
        where = pl.ds(pl.multiple_of((h + 1) * pair, pair), pair)
        base[:, where, :channels] = spectrum[0]
        base[:, where, channels:] = spectrum[1]
        return carry

    lax.fori_loop(0, side, analyse, 0, unroll=4)
    base[:, :pair] = base[:, rows : rows + pair]
    base[:, rows + pair :] = base[:, pair : 2 * pair]

    def apply(source, weight):
        stacked = jnp.concatenate([source[2 * pair :], source[pair : rows + pair], source[:rows]], axis=1)
        return jnp.dot(stacked, weight, preferred_element_type=jnp.float32)

    def slot_group(index, carry):
        slots = [index * group + lane for lane in range(group)]
        for lane, slot in enumerate(slots):
            cos_a, cos_b, sine = slot_table[0, slot], slot_table[1, slot], slot_table[2, slot]
            for row in range(3):
                turned = (sine * mixes[row, 2]).astype(jnp.bfloat16)
                lo, hi = row * wide, row * wide + channels
                weights[lane, lo:hi, :channels] = (mixes[row, 0] + cos_a * mixes[row, 1]).astype(jnp.bfloat16)
                weights[lane, hi : hi + channels, channels:] = (mixes[row, 0] + cos_b * mixes[row, 1]).astype(jnp.bfloat16)
                weights[lane, lo:hi, channels:] = turned
                weights[lane, hi : hi + channels, :channels] = -turned
        powers = 2 ** (NS_STEPS + 1) - 1
        for step in range(powers):
            for lane, slot in enumerate(slots):
                source = base.at[slot] if step == 0 else (state if step % 2 else other).at[lane]
                target = (other if step % 2 else state).at[lane]
                product = apply(source, weights[lane]).reshape(side, 2, images, wide)
                start = base[slot, pair : rows + pair].astype(jnp.float32).reshape(side, 2, images, wide)
                forward = start[:, 0] - product[:, 0]
                backward = start[:, 1] + product[:, 1]
                joined = jnp.stack([forward, backward], axis=1).reshape(rows, wide).astype(jnp.bfloat16)
                target[pair : rows + pair] = joined
                if step < powers - 1:
                    target[:pair] = joined[rows - pair :]
                    target[rows + pair :] = joined[:pair]
                else:
                    finished = (2.0 / GAIN**2) * forward - (1.0 / GAIN**2) * start[:, 0]
                    answer[slot] = finished.reshape(side * images, wide)
                    crossed = jnp.stack([-backward, forward], axis=1).reshape(rows, wide).astype(jnp.bfloat16)
                    partner[lane, pair:] = crossed
                    partner[lane, :pair] = crossed[rows - pair :]
        last = state if powers % 2 else other
        for lane, slot in enumerate(slots):
            cos_a, cos_b, sine, scale = (slot_table[k, slot] for k in range(4))
            left = last[lane, pair : rows + pair]
            for row, right in enumerate((partner[lane, pair:], partner[lane, :rows])):
                outer = lax.dot_general(left, right, (((0,), (0,)), ((), ())), preferred_element_type=jnp.float32)
                outer = outer * scale
                first, second = outer[:channels, :channels], outer[channels:, channels:]
                total[row, 0] += first + second
                total[row, 1] += cos_a * first + cos_b * second
                total[row, 2] += sine * (outer[channels:, :channels] - outer[:channels, channels:])
        return carry

    lax.fori_loop(0, half // group, slot_group, 0)

    def lay(place, piece):
        chunks[:, :, place] = piece.reshape(2, chips, channels)

    lay(0, total[0, 0])
    lay(1, total[0, 1] - total[0, 2])
    lay(2, total[1, 0])
    lay(3, total[1, 1] - total[1, 2])
    lay(4, total[1, 1] + total[1, 2])
    pl.semaphore_wait(barrier, chips)
    swap = remote(chunks.at[1 - core], from_partner, core_sem.at[0], core_sem.at[1], chip, 1 - core)
    swap.start()
    loads[4].wait()

    def synthesise(index, carry):
        columns = []
        for part in range(2):
            where = pl.ds(pl.multiple_of((2 * index + part) * images, images), images)
            tiles = [answer[:, where, k * channels : (k + 1) * channels].reshape(half * images, channels) for k in range(2)]
            columns.append(jnp.concatenate(tiles, axis=0).astype(jnp.bfloat16))
        maps = jnp.dot(synthesis[...], jnp.concatenate(columns, axis=1), preferred_element_type=jnp.float32)
        maps = maps.astype(jnp.bfloat16)
        for part in range(2):
            result[:, 2 * index + part] = maps[:, part * channels : (part + 1) * channels].reshape(images, side, channels)
        return carry

    third = side // 6
    lax.fori_loop(0, third, synthesise, 0, unroll=True)
    swap.wait()
    mine[...] = chunks[core] + from_partner[...]

    def scatter(ahead, carry):
        there = (chip + ahead) % chips
        remote(mine.at[there], received.at[ahead - 1], chip_send.at[0], chip_recv.at[0], there, core).start()
        return carry

    lax.fori_loop(1, chips, scatter, 0)
    lax.fori_loop(third, 2 * third, synthesise, 0, unroll=True)
    everything = pltpu.make_async_copy(received, received, chip_recv.at[0])
    everything.wait()
    pltpu.make_async_copy(received, received, chip_send.at[0]).wait()
    gathered[core, chip] = mine[chip] + jnp.sum(received[...], axis=0)

    def spread(ahead, carry):
        there = (chip + ahead) % chips
        piece = gathered.at[core, chip]
        remote(piece, piece, chip_send.at[1], chip_recv.at[1], there, core).start()
        return carry

    lax.fori_loop(1, chips, spread, 0)
    lax.fori_loop(2 * third, side // 2, synthesise, 0, unroll=True)
    store = pltpu.make_async_copy(result, outputs_hbm, out_sem)
    store.start()
    pltpu.make_async_copy(received, received, chip_recv.at[1]).wait()
    pltpu.make_async_copy(received, received, chip_send.at[1]).wait()
    ours = gathered.at[core]
    swap = remote(ours, ours, core_sem.at[2], core_sem.at[3], chip, 1 - core)
    swap.start()
    swap.wait()

    sums = [gathered[:, :, place].reshape(channels, channels) for place in range(5)]
    for place, (row, col) in enumerate(((1, 1), (1, 2), (2, 1), (2, 2), (2, 0))):
        kernel_grad[row, col] = sums[place]
        if place:
            kernel_grad[2 - row, 2 - col] = -sums[place].T
    store.wait()


def layer(pictures, cotangent, kernel, total_images, group=2):
    images, side, _, channels = pictures.shape
    half = side // 2
    pair = 2 * images
    rows = side * pair
    wide = 2 * channels
    analysis, synthesis = transform_tables(side, images)
    analysis = jnp.asarray(analysis, jnp.bfloat16)
    synthesis = jnp.asarray(synthesis, jnp.bfloat16)
    table = jnp.asarray(slot_tables(side, total_images))
    anywhere = pl.BlockSpec(memory_space=pltpu.HBM)
    chips = lax.axis_size("sample") * lax.axis_size("freq") // 2
    return pl.pallas_call(
        functools.partial(layer_kernel, images, channels, side, group),
        out_shape=(
            jax.ShapeDtypeStruct(pictures.shape, jnp.bfloat16),
            jax.ShapeDtypeStruct(kernel.shape, jnp.float32),
        ),
        in_specs=[pl.BlockSpec(memory_space=pltpu.SMEM)] + [anywhere] * 5,
        out_specs=(anywhere, pl.BlockSpec(memory_space=pltpu.VMEM)),
        scratch_shapes=[
            pltpu.VMEM(pictures.shape, jnp.bfloat16),
            pltpu.VMEM(pictures.shape, jnp.bfloat16),
            pltpu.VMEM(kernel.shape, jnp.float32),
            pltpu.VMEM((wide, wide), jnp.bfloat16),
            pltpu.VMEM((wide, wide), jnp.bfloat16),
            pltpu.VMEM((3, 3, channels, channels), jnp.float32),
            pltpu.VMEM((group, 3 * wide, wide), jnp.bfloat16),
            pltpu.VMEM((half, rows + 2 * pair, wide), jnp.bfloat16),
            pltpu.VMEM((group, rows + 2 * pair, wide), jnp.bfloat16),
            pltpu.VMEM((group, rows + 2 * pair, wide), jnp.bfloat16),
            pltpu.VMEM((group, rows + pair, wide), jnp.bfloat16),
            pltpu.VMEM((half, side * images, wide), jnp.float32),
            pltpu.VMEM((2, 3, channels, channels), jnp.float32),
            pltpu.VMEM(pictures.shape, jnp.bfloat16),
            pltpu.VMEM((2, chips, 5, channels), jnp.float32),
            pltpu.VMEM((chips, 5, channels), jnp.float32),
            pltpu.VMEM((chips, 5, channels), jnp.float32),
            pltpu.VMEM((chips - 1, 5, channels), jnp.float32),
            pltpu.VMEM((2, chips, 5, channels), jnp.float32),
            pltpu.SemaphoreType.DMA((5,)),
            pltpu.SemaphoreType.DMA,
            pltpu.SemaphoreType.DMA((4,)),
            pltpu.SemaphoreType.DMA((2,)),
            pltpu.SemaphoreType.DMA((2,)),
        ],
        compiler_params=pltpu.CompilerParams(vmem_limit_bytes=63 * 1024 * 1024, collective_id=0, has_side_effects=True),
        name="layer",
    )(table, pictures, cotangent, kernel, analysis, synthesis)


def per_device(images, cotangent, kernel):
    total = images.shape[0] * lax.axis_size("sample") * lax.axis_size("freq")
    return layer(images, cotangent, kernel, total)


def solution(mesh):
    placed = P(("sample", "freq"), None, None, None)
    return jax.shard_map(
        per_device,
        mesh=mesh,
        in_specs=(placed, placed, P()),
        out_specs=(placed, P()),
        check_vma=False,
    )
```

```python
import functools
import math

import jax
import jax.numpy as jnp
import numpy as np
from jax import lax
from jax.experimental import pallas as pl
from jax.experimental.pallas import tpu as pltpu
from jax.sharding import PartitionSpec as P

NS_STEPS = 2
GAIN = 1.6245


def transform_tables(side, images):
    half = side // 2
    freq = np.arange(half)
    cell = np.arange(side)
    angle = 2.0 * math.pi / side * ((freq[:, None] * cell[None, :]) % side)
    real_rows = np.cos(angle)
    imag_rows = -np.sin(angle)
    imag_rows[0] = np.where(cell % 2 == 0, 1.0, -1.0)
    forward = np.stack([real_rows, imag_rows])
    weight = np.full((2, half, 1), 2.0 / side)
    weight[:, 0] = 1.0 / side
    same = np.eye(images)
    analysis = np.einsum("asw,nm->asnmw", forward, same).reshape(side * images, images * side)
    synthesis = np.einsum("asw,nm->nwasm", forward * weight, same).reshape(images * side, side * images)
    return GAIN * analysis, GAIN * synthesis


def slot_tables(side, total_images):
    half = side // 2
    angle = 2.0 * math.pi / side * np.arange(half)
    cos_a, cos_b, sine = np.cos(angle), np.cos(angle), np.sin(angle)
    cos_b[0] = -1.0
    sine[0] = 0.0
    scale = np.full(half, -2.0 * 2.0 / (total_images * side * GAIN**2))
    scale[0] *= 0.5
    return np.stack([cos_a, cos_b, sine, scale]).astype(np.float32)


def hops(ahead, ring):
    x = 2 * (ahead & 1) + ahead // ring
    return sum((0, 1, 2, 1)[part] for part in (x, ahead // 8 % 4, ahead // 2 % 4))


def layer_kernel(
    images, channels, side, group, slot_table, pictures_hbm, cotangent_hbm, taps_hbm, analysis_hbm, synthesis_hbm,
    outputs_hbm, kernel_grad,
    pictures, cotangent, taps, analysis, synthesis, mixes, weights, base, state, other, partner, answer, total,
    result, chunks, from_partner, mine, received, gathered, in_sem, out_sem, core_sem, chip_send, chip_recv,
):
    half = side // 2
    pair = 2 * images
    rows = side * pair
    wide = 2 * channels
    sample, freq = lax.axis_index("sample"), lax.axis_index("freq")
    ring = lax.axis_size("freq")
    chips = lax.axis_size("sample") * ring // 2
    core = sample % 2
    chip = sample // 2 * ring + freq

    def place_of(to_chip, to_core):
        return (to_chip // ring * 2 + to_core, to_chip % ring)

    def remote(source, target, send, recv, to_chip, to_core):
        return pltpu.make_async_remote_copy(
            source, target, send, recv, device_id=place_of(to_chip, to_core), device_id_type=pl.DeviceIdType.MESH
        )

    barrier = pltpu.get_barrier_semaphore()
    far_first = sorted(range(1, chips), key=lambda ahead: -hops(ahead, ring))

    loads = [
        pltpu.make_async_copy(taps_hbm, taps, in_sem.at[0]),
        pltpu.make_async_copy(analysis_hbm, analysis, in_sem.at[1]),
        pltpu.make_async_copy(pictures_hbm, pictures, in_sem.at[2]),
        pltpu.make_async_copy(cotangent_hbm, cotangent, in_sem.at[3]),
        pltpu.make_async_copy(synthesis_hbm, synthesis, in_sem.at[4]),
    ]
    for load in loads:
        load.start()
    loads[0].wait()
    for row in range(3):
        across = [taps[row, col].T - taps[2 - row, 2 - col] for col in range(3)]
        mixes[row, 0] = across[1]
        mixes[row, 1] = across[2] + across[0]
        mixes[row, 2] = across[0] - across[2]
    total[...] = jnp.zeros_like(total)

    def greet(beside, carry):
        there = place_of(chip ^ beside, jnp.where(beside == 0, 1 - core, core))
        pl.semaphore_signal(barrier, inc=1, device_id=there, device_id_type=pl.DeviceIdType.MESH)
        return carry

    lax.fori_loop(0, chips, greet, 0, unroll=8)
    for load in loads[1:4]:
        load.wait()

    def analyse(h, carry):
        both = jnp.concatenate(
            [pictures[:, h].reshape(images * side, channels), cotangent[:, h].reshape(images * side, channels)], axis=1
        )
        spectrum = jnp.dot(analysis[...], both, preferred_element_type=jnp.float32)
        spectrum = spectrum.reshape(2, half, images, wide)
        spectrum = jnp.concatenate([spectrum[..., :channels], spectrum[..., channels:]], axis=2).astype(jnp.bfloat16)
        where = pl.ds(pl.multiple_of((h + 1) * pair, pair), pair)
        base[:, where, :channels] = spectrum[0]
        base[:, where, channels:] = spectrum[1]
        return carry

    lax.fori_loop(0, side, analyse, 0, unroll=4)
    base[:, :pair] = base[:, rows : rows + pair]
    base[:, rows + pair :] = base[:, pair : 2 * pair]

    def apply(source, weight):
        stacked = jnp.concatenate([source[2 * pair :], source[pair : rows + pair], source[:rows]], axis=1)
        return jnp.dot(stacked, weight, preferred_element_type=jnp.float32)

    powers = 2 ** (NS_STEPS + 1) - 1
    last = state if powers % 2 else other

    def weigh(lane, slot):
        cos_a, cos_b, sine = slot_table[0, slot], slot_table[1, slot], slot_table[2, slot]
        for row in range(3):
            turned = (sine * mixes[row, 2]).astype(jnp.bfloat16)
            lo, hi = row * wide, row * wide + channels
            weights[lane, lo:hi, :channels] = (mixes[row, 0] + cos_a * mixes[row, 1]).astype(jnp.bfloat16)
            weights[lane, hi : hi + channels, channels:] = (mixes[row, 0] + cos_b * mixes[row, 1]).astype(jnp.bfloat16)
            weights[lane, lo:hi, channels:] = turned
            weights[lane, hi : hi + channels, :channels] = -turned

    def power(lane, slot, step):
        source = base.at[slot] if step == 0 else (state if step % 2 else other).at[lane]
        target = (other if step % 2 else state).at[lane]
        product = apply(source, weights[lane]).reshape(side, 2, images, wide)
        start = base[slot, pair : rows + pair].astype(jnp.float32).reshape(side, 2, images, wide)
        forward = start[:, 0] - product[:, 0]
        backward = start[:, 1] + product[:, 1]
        joined = jnp.stack([forward, backward], axis=1).reshape(rows, wide).astype(jnp.bfloat16)
        target[pair : rows + pair] = joined
        if step < powers - 1:
            target[:pair] = joined[rows - pair :]
            target[rows + pair :] = joined[:pair]
        else:
            finished = (2.0 / GAIN**2) * forward - (1.0 / GAIN**2) * start[:, 0]
            answer[slot] = finished.reshape(side * images, wide)
            crossed = jnp.stack([-backward, forward], axis=1).reshape(rows, wide).astype(jnp.bfloat16)
            partner[lane, pair:] = crossed
            partner[lane, :pair] = crossed[rows - pair :]

    def correlate(lane, slot):
        cos_a, cos_b, sine, scale = (slot_table[k, slot] for k in range(4))
        left = last[lane, pair : rows + pair]
        for row, right in enumerate((partner[lane, pair:], partner[lane, :rows])):
            outer = lax.dot_general(left, right, (((0,), (0,)), ((), ())), preferred_element_type=jnp.float32)
            outer = outer * scale
            first, second = outer[:channels, :channels], outer[channels:, channels:]
            total[row, 0] += first + second
            total[row, 1] += cos_a * first + cos_b * second
            total[row, 2] += sine * (outer[channels:, :channels] - outer[:channels, channels:])

    early, late = (0, 1), (2, 3)
    for lane in early:
        weigh(lane, lane)
    for lane in late:
        last[lane] = jnp.zeros_like(last[lane])
        partner[lane] = jnp.zeros_like(partner[lane])

    def slot_group(index, carry):
        slot = [index * group + lane for lane in range(group)]
        before = [jnp.maximum(slot[lane] - group, 0) for lane in range(group)]
        after = [jnp.minimum(slot[lane] + group, half - 1) for lane in range(group)]
        for lane in early:
            power(lane, slot[lane], 0)
            correlate(lane + 2, before[lane + 2])
        for step in range(1, powers - 1):
            for lane in early:
                power(lane, slot[lane], step)
                if step == 2:
                    weigh(lane + 2, slot[lane + 2])
        for lane in early:
            power(lane + 2, slot[lane + 2], 0)
            power(lane, slot[lane], powers - 1)
        for lane in early:
            power(lane + 2, slot[lane + 2], 1)
            correlate(lane, slot[lane])
        for step in range(2, powers):
            for lane in late:
                power(lane, slot[lane], step)
                if step == 3:
                    weigh(lane - 2, after[lane - 2])
        return carry

    lax.fori_loop(0, half // group, slot_group, 0)
    for lane in late:
        correlate(lane, half - group + lane)

    def lay(place, piece):
        chunks[:, :, place] = piece.reshape(2, chips, channels)

    lay(0, total[0, 0])
    lay(1, total[0, 1] - total[0, 2])
    lay(2, total[1, 0])
    lay(3, total[1, 1] - total[1, 2])
    lay(4, total[1, 1] + total[1, 2])
    pl.semaphore_wait(barrier, chips)
    swap = remote(chunks.at[1 - core], from_partner, core_sem.at[0], core_sem.at[1], chip, 1 - core)
    swap.start()
    loads[4].wait()

    def synthesise(index, carry):
        columns = []
        for part in range(2):
            where = pl.ds(pl.multiple_of((2 * index + part) * images, images), images)
            tiles = [answer[:, where, k * channels : (k + 1) * channels].reshape(half * images, channels) for k in range(2)]
            columns.append(jnp.concatenate(tiles, axis=0).astype(jnp.bfloat16))
        maps = jnp.dot(synthesis[...], jnp.concatenate(columns, axis=1), preferred_element_type=jnp.float32)
        maps = maps.astype(jnp.bfloat16)
        for part in range(2):
            result[:, 2 * index + part] = maps[:, part * channels : (part + 1) * channels].reshape(images, side, channels)
        return carry

    third = side // 6
    lax.fori_loop(0, third, synthesise, 0, unroll=True)
    swap.wait()
    mine[...] = chunks[core] + from_partner[...]

    for ahead in far_first:
        there = chip ^ ahead
        remote(mine.at[there], received.at[ahead - 1], chip_send.at[0], chip_recv.at[0], there, core).start()
    lax.fori_loop(third, 2 * third, synthesise, 0, unroll=True)
    everything = pltpu.make_async_copy(received, received, chip_recv.at[0])
    everything.wait()
    pltpu.make_async_copy(received, received, chip_send.at[0]).wait()
    gathered[core, chip] = mine[chip] + jnp.sum(received[...], axis=0)

    piece = gathered.at[core, chip]
    for ahead in far_first:
        remote(piece, piece, chip_send.at[1], chip_recv.at[1], chip ^ ahead, core).start()
    lax.fori_loop(2 * third, side // 2, synthesise, 0, unroll=True)
    store = pltpu.make_async_copy(result, outputs_hbm, out_sem)
    store.start()
    pltpu.make_async_copy(received, received, chip_recv.at[1]).wait()
    pltpu.make_async_copy(received, received, chip_send.at[1]).wait()
    ours = gathered.at[core]
    swap = remote(ours, ours, core_sem.at[2], core_sem.at[3], chip, 1 - core)
    swap.start()
    swap.wait()

    sums = [gathered[:, :, place].reshape(channels, channels) for place in range(5)]
    for place, (row, col) in enumerate(((1, 1), (1, 2), (2, 1), (2, 2), (2, 0))):
        kernel_grad[row, col] = sums[place]
        if place:
            kernel_grad[2 - row, 2 - col] = -sums[place].T
    store.wait()


def layer(pictures, cotangent, kernel, total_images, group=4):
    images, side, _, channels = pictures.shape
    half = side // 2
    pair = 2 * images
    rows = side * pair
    wide = 2 * channels
    analysis, synthesis = transform_tables(side, images)
    analysis = jnp.asarray(analysis, jnp.bfloat16)
    synthesis = jnp.asarray(synthesis, jnp.bfloat16)
    table = jnp.asarray(slot_tables(side, total_images))
    anywhere = pl.BlockSpec(memory_space=pltpu.HBM)
    chips = lax.axis_size("sample") * lax.axis_size("freq") // 2
    return pl.pallas_call(
        functools.partial(layer_kernel, images, channels, side, group),
        out_shape=(
            jax.ShapeDtypeStruct(pictures.shape, jnp.bfloat16),
            jax.ShapeDtypeStruct(kernel.shape, jnp.float32),
        ),
        in_specs=[pl.BlockSpec(memory_space=pltpu.SMEM)] + [anywhere] * 5,
        out_specs=(anywhere, pl.BlockSpec(memory_space=pltpu.VMEM)),
        scratch_shapes=[
            pltpu.VMEM(pictures.shape, jnp.bfloat16),
            pltpu.VMEM(pictures.shape, jnp.bfloat16),
            pltpu.VMEM(kernel.shape, jnp.float32),
            pltpu.VMEM((wide, wide), jnp.bfloat16),
            pltpu.VMEM((wide, wide), jnp.bfloat16),
            pltpu.VMEM((3, 3, channels, channels), jnp.float32),
            pltpu.VMEM((group, 3 * wide, wide), jnp.bfloat16),
            pltpu.VMEM((half, rows + 2 * pair, wide), jnp.bfloat16),
            pltpu.VMEM((group, rows + 2 * pair, wide), jnp.bfloat16),
            pltpu.VMEM((group, rows + 2 * pair, wide), jnp.bfloat16),
            pltpu.VMEM((group, rows + pair, wide), jnp.bfloat16),
            pltpu.VMEM((half, side * images, wide), jnp.float32),
            pltpu.VMEM((2, 3, channels, channels), jnp.float32),
            pltpu.VMEM(pictures.shape, jnp.bfloat16),
            pltpu.VMEM((2, chips, 5, channels), jnp.float32),
            pltpu.VMEM((chips, 5, channels), jnp.float32),
            pltpu.VMEM((chips, 5, channels), jnp.float32),
            pltpu.VMEM((chips - 1, 5, channels), jnp.float32),
            pltpu.VMEM((2, chips, 5, channels), jnp.float32),
            pltpu.SemaphoreType.DMA((5,)),
            pltpu.SemaphoreType.DMA,
            pltpu.SemaphoreType.DMA((4,)),
            pltpu.SemaphoreType.DMA((2,)),
            pltpu.SemaphoreType.DMA((2,)),
        ],
        compiler_params=pltpu.CompilerParams(vmem_limit_bytes=63 * 1024 * 1024, collective_id=0, has_side_effects=True),
        name="layer",
    )(table, pictures, cotangent, kernel, analysis, synthesis)


def per_device(images, cotangent, kernel):
    total = images.shape[0] * lax.axis_size("sample") * lax.axis_size("freq")
    return layer(images, cotangent, kernel, total)


def solution(mesh):
    placed = P(("sample", "freq"), None, None, None)
    return jax.shard_map(
        per_device,
        mesh=mesh,
        in_specs=(placed, placed, P()),
        out_specs=(placed, P()),
        check_vma=False,
    )
```

```python
import functools
import math

import jax
import jax.numpy as jnp
import numpy as np
from jax import lax
from jax.experimental import pallas as pl
from jax.experimental.pallas import tpu as pltpu
from jax.sharding import PartitionSpec as P

NS_STEPS = 2
GAIN = 1.6245


def transform_tables(side, images):
    half = side // 2
    freq = np.arange(half)
    cell = np.arange(side)
    angle = 2.0 * math.pi / side * ((freq[:, None] * cell[None, :]) % side)
    real_rows = np.cos(angle)
    imag_rows = -np.sin(angle)
    imag_rows[0] = np.where(cell % 2 == 0, 1.0, -1.0)
    forward = np.stack([real_rows, imag_rows])
    weight = np.full((2, half, 1), 2.0 / side)
    weight[:, 0] = 1.0 / side
    same = np.eye(images)
    analysis = np.einsum("asw,nm->asnmw", forward, same).reshape(side * images, images * side)
    synthesis = np.einsum("asw,nm->nwasm", forward * weight, same).reshape(images * side, side * images)
    return GAIN * analysis, GAIN * synthesis


def slot_tables(side, total_images):
    half = side // 2
    angle = 2.0 * math.pi / side * np.arange(half)
    cos_a, cos_b, sine = np.cos(angle), np.cos(angle), np.sin(angle)
    cos_b[0] = -1.0
    sine[0] = 0.0
    scale = np.full(half, -2.0 * 2.0 / (total_images * side * GAIN**2))
    scale[0] *= 0.5
    return np.stack([cos_a, cos_b, sine, scale]).astype(np.float32)


def hops(ahead, ring):
    x = 2 * (ahead & 1) + ahead // ring
    return sum((0, 1, 2, 1)[part] for part in (x, ahead // 8 % 4, ahead // 2 % 4))


def layer_kernel(
    images, channels, side, group, slot_table, pictures_hbm, cotangent_hbm, taps_hbm, analysis_hbm, synthesis_hbm,
    result, kernel_grad,
    pictures, cotangent, taps, analysis, synthesis, mixes, weights, base, state, other, partner, answer, total,
    chunks, from_partner, mine, received, gathered, in_sem, core_sem, chip_send, chip_recv,
):
    half = side // 2
    pair = 2 * images
    rows = side * pair
    wide = 2 * channels
    sample, freq = lax.axis_index("sample"), lax.axis_index("freq")
    ring = lax.axis_size("freq")
    chips = lax.axis_size("sample") * ring // 2
    core = sample % 2
    chip = sample // 2 * ring + freq

    def place_of(to_chip, to_core):
        return (to_chip // ring * 2 + to_core, to_chip % ring)

    def remote(source, target, send, recv, to_chip, to_core):
        return pltpu.make_async_remote_copy(
            source, target, send, recv, device_id=place_of(to_chip, to_core), device_id_type=pl.DeviceIdType.MESH
        )

    barrier = pltpu.get_barrier_semaphore()
    far_first = sorted(range(1, chips), key=lambda ahead: -hops(ahead, ring))

    loads = [
        pltpu.make_async_copy(taps_hbm, taps, in_sem.at[0]),
        pltpu.make_async_copy(analysis_hbm, analysis, in_sem.at[1]),
        pltpu.make_async_copy(pictures_hbm, pictures, in_sem.at[2]),
        pltpu.make_async_copy(cotangent_hbm, cotangent, in_sem.at[3]),
        pltpu.make_async_copy(synthesis_hbm, synthesis, in_sem.at[4]),
    ]
    for load in loads:
        load.start()
    loads[0].wait()
    for row in range(3):
        across = [taps[row, col].T - taps[2 - row, 2 - col] for col in range(3)]
        mixes[row, 0] = across[1]
        mixes[row, 1] = across[2] + across[0]
        mixes[row, 2] = across[0] - across[2]
    total[...] = jnp.zeros_like(total)

    def greet(beside, carry):
        there = place_of(chip ^ beside, jnp.where(beside == 0, 1 - core, core))
        pl.semaphore_signal(barrier, inc=1, device_id=there, device_id_type=pl.DeviceIdType.MESH)
        return carry

    lax.fori_loop(0, chips, greet, 0, unroll=8)
    for load in loads[1:4]:
        load.wait()

    def analyse(h, carry):
        both = jnp.concatenate(
            [pictures[:, h].reshape(images * side, channels), cotangent[:, h].reshape(images * side, channels)], axis=1
        )
        spectrum = jnp.dot(analysis[...], both, preferred_element_type=jnp.float32)
        spectrum = spectrum.reshape(2, half, images, wide)
        spectrum = jnp.concatenate([spectrum[..., :channels], spectrum[..., channels:]], axis=2).astype(jnp.bfloat16)
        where = pl.ds(pl.multiple_of((h + 1) * pair, pair), pair)
        base[:, where, :channels] = spectrum[0]
        base[:, where, channels:] = spectrum[1]
        return carry

    lax.fori_loop(0, side, analyse, 0, unroll=4)
    base[:, :pair] = base[:, rows : rows + pair]
    base[:, rows + pair :] = base[:, pair : 2 * pair]

    def apply(source, weight):
        stacked = jnp.concatenate([source[2 * pair :], source[pair : rows + pair], source[:rows]], axis=1)
        return jnp.dot(stacked, weight, preferred_element_type=jnp.float32)

    powers = 2 ** (NS_STEPS + 1) - 1
    last = state if powers % 2 else other

    def weigh(lane, slot):
        cos_a, cos_b, sine = slot_table[0, slot], slot_table[1, slot], slot_table[2, slot]
        for row in range(3):
            turned = (sine * mixes[row, 2]).astype(jnp.bfloat16)
            lo, hi = row * wide, row * wide + channels
            weights[lane, lo:hi, :channels] = (mixes[row, 0] + cos_a * mixes[row, 1]).astype(jnp.bfloat16)
            weights[lane, hi : hi + channels, channels:] = (mixes[row, 0] + cos_b * mixes[row, 1]).astype(jnp.bfloat16)
            weights[lane, lo:hi, channels:] = turned
            weights[lane, hi : hi + channels, :channels] = -turned

    def power(lane, slot, step):
        source = base.at[slot] if step == 0 else (state if step % 2 else other).at[lane]
        target = (other if step % 2 else state).at[lane]
        product = apply(source, weights[lane]).reshape(side, 2, images, wide)
        start = base[slot, pair : rows + pair].astype(jnp.float32).reshape(side, 2, images, wide)
        forward = start[:, 0] - product[:, 0]
        backward = start[:, 1] + product[:, 1]
        joined = jnp.stack([forward, backward], axis=1).reshape(rows, wide).astype(jnp.bfloat16)
        target[pair : rows + pair] = joined
        if step < powers - 1:
            target[:pair] = joined[rows - pair :]
            target[rows + pair :] = joined[:pair]
        else:
            finished = (2.0 / GAIN**2) * forward - (1.0 / GAIN**2) * start[:, 0]
            answer[slot] = finished.reshape(side * images, wide)
            crossed = jnp.stack([-backward, forward], axis=1).reshape(rows, wide).astype(jnp.bfloat16)
            partner[lane, pair:] = crossed
            partner[lane, :pair] = crossed[rows - pair :]

    def correlate(lane, slot):
        cos_a, cos_b, sine, scale = (slot_table[k, slot] for k in range(4))
        left = last[lane, pair : rows + pair]
        for row, right in enumerate((partner[lane, pair:], partner[lane, :rows])):
            outer = lax.dot_general(left, right, (((0,), (0,)), ((), ())), preferred_element_type=jnp.float32)
            outer = outer * scale
            first, second = outer[:channels, :channels], outer[channels:, channels:]
            total[row, 0] += first + second
            total[row, 1] += cos_a * first + cos_b * second
            total[row, 2] += sine * (outer[channels:, :channels] - outer[:channels, channels:])

    early, late = (0, 1), (2, 3)
    for lane in early:
        weigh(lane, lane)
    for lane in late:
        last[lane] = jnp.zeros_like(last[lane])
        partner[lane] = jnp.zeros_like(partner[lane])

    def slot_group(index, carry):
        slot = [index * group + lane for lane in range(group)]
        before = [jnp.maximum(slot[lane] - group, 0) for lane in range(group)]
        after = [jnp.minimum(slot[lane] + group, half - 1) for lane in range(group)]
        for lane in early:
            power(lane, slot[lane], 0)
            correlate(lane + 2, before[lane + 2])
        for step in range(1, powers - 1):
            for lane in early:
                power(lane, slot[lane], step)
                if step == 2:
                    weigh(lane + 2, slot[lane + 2])
        for lane in early:
            power(lane + 2, slot[lane + 2], 0)
            power(lane, slot[lane], powers - 1)
        for lane in early:
            power(lane + 2, slot[lane + 2], 1)
            correlate(lane, slot[lane])
        for step in range(2, powers):
            for lane in late:
                power(lane, slot[lane], step)
                if step == 3:
                    weigh(lane - 2, after[lane - 2])
        return carry

    lax.fori_loop(0, half // group, slot_group, 0)
    for lane in late:
        correlate(lane, half - group + lane)

    def lay(place, piece):
        chunks[:, :, place] = piece.reshape(2, chips, channels)

    lay(0, total[0, 0])
    lay(1, total[0, 1] - total[0, 2])
    lay(2, total[1, 0])
    lay(3, total[1, 1] - total[1, 2])
    lay(4, total[1, 1] + total[1, 2])
    pl.semaphore_wait(barrier, chips)
    swap = remote(chunks.at[1 - core], from_partner, core_sem.at[0], core_sem.at[1], chip, 1 - core)
    swap.start()
    loads[4].wait()

    def synthesise(index, carry):
        columns = []
        for part in range(2):
            where = pl.ds(pl.multiple_of((2 * index + part) * images, images), images)
            tiles = [answer[:, where, k * channels : (k + 1) * channels].reshape(half * images, channels) for k in range(2)]
            columns.append(jnp.concatenate(tiles, axis=0).astype(jnp.bfloat16))
        maps = jnp.dot(synthesis[...], jnp.concatenate(columns, axis=1), preferred_element_type=jnp.float32)
        maps = maps.astype(jnp.bfloat16)
        for part in range(2):
            result[:, 2 * index + part] = maps[:, part * channels : (part + 1) * channels].reshape(images, side, channels)
        return carry

    third = side // 6
    lax.fori_loop(0, third, synthesise, 0, unroll=True)
    swap.wait()
    mine[...] = chunks[core] + from_partner[...]

    for ahead in far_first:
        there = chip ^ ahead
        remote(mine.at[there], received.at[ahead - 1], chip_send.at[0], chip_recv.at[0], there, core).start()
    lax.fori_loop(third, 2 * third, synthesise, 0, unroll=True)
    everything = pltpu.make_async_copy(received, received, chip_recv.at[0])
    everything.wait()
    pltpu.make_async_copy(received, received, chip_send.at[0]).wait()
    gathered[core, chip] = mine[chip] + jnp.sum(received[...], axis=0)

    piece = gathered.at[core, chip]
    for ahead in far_first:
        remote(piece, piece, chip_send.at[1], chip_recv.at[1], chip ^ ahead, core).start()
    lax.fori_loop(2 * third, side // 2, synthesise, 0, unroll=True)
    pltpu.make_async_copy(received, received, chip_recv.at[1]).wait()
    pltpu.make_async_copy(received, received, chip_send.at[1]).wait()
    ours = gathered.at[core]
    swap = remote(ours, ours, core_sem.at[2], core_sem.at[3], chip, 1 - core)
    swap.start()
    swap.wait()

    sums = [gathered[:, :, place].reshape(channels, channels) for place in range(5)]
    for place, (row, col) in enumerate(((1, 1), (1, 2), (2, 1), (2, 2), (2, 0))):
        kernel_grad[row, col] = sums[place]
        if place:
            kernel_grad[2 - row, 2 - col] = -sums[place].T


def layer(pictures, cotangent, kernel, total_images, group=4):
    images, side, _, channels = pictures.shape
    half = side // 2
    pair = 2 * images
    rows = side * pair
    wide = 2 * channels
    analysis, synthesis = transform_tables(side, images)
    analysis = jnp.asarray(analysis, jnp.bfloat16)
    synthesis = jnp.asarray(synthesis, jnp.bfloat16)
    table = jnp.asarray(slot_tables(side, total_images))
    anywhere = pl.BlockSpec(memory_space=pltpu.HBM)
    chips = lax.axis_size("sample") * lax.axis_size("freq") // 2
    return pl.pallas_call(
        functools.partial(layer_kernel, images, channels, side, group),
        out_shape=(
            pltpu.VMEM(pictures.shape, jnp.bfloat16),
            pltpu.VMEM(kernel.shape, jnp.float32),
        ),
        in_specs=[pl.BlockSpec(memory_space=pltpu.SMEM)] + [anywhere] * 5,
        out_specs=(pl.BlockSpec(memory_space=pltpu.VMEM), pl.BlockSpec(memory_space=pltpu.VMEM)),
        scratch_shapes=[
            pltpu.VMEM(pictures.shape, jnp.bfloat16),
            pltpu.VMEM(pictures.shape, jnp.bfloat16),
            pltpu.VMEM(kernel.shape, jnp.float32),
            pltpu.VMEM((wide, wide), jnp.bfloat16),
            pltpu.VMEM((wide, wide), jnp.bfloat16),
            pltpu.VMEM((3, 3, channels, channels), jnp.float32),
            pltpu.VMEM((group, 3 * wide, wide), jnp.bfloat16),
            pltpu.VMEM((half, rows + 2 * pair, wide), jnp.bfloat16),
            pltpu.VMEM((group, rows + 2 * pair, wide), jnp.bfloat16),
            pltpu.VMEM((group, rows + 2 * pair, wide), jnp.bfloat16),
            pltpu.VMEM((group, rows + pair, wide), jnp.bfloat16),
            pltpu.VMEM((half, side * images, wide), jnp.float32),
            pltpu.VMEM((2, 3, channels, channels), jnp.float32),
            pltpu.VMEM((2, chips, 5, channels), jnp.float32),
            pltpu.VMEM((chips, 5, channels), jnp.float32),
            pltpu.VMEM((chips, 5, channels), jnp.float32),
            pltpu.VMEM((chips - 1, 5, channels), jnp.float32),
            pltpu.VMEM((2, chips, 5, channels), jnp.float32),
            pltpu.SemaphoreType.DMA((5,)),
            pltpu.SemaphoreType.DMA((4,)),
            pltpu.SemaphoreType.DMA((2,)),
            pltpu.SemaphoreType.DMA((2,)),
        ],
        compiler_params=pltpu.CompilerParams(vmem_limit_bytes=60 * 1024 * 1024, collective_id=0, has_side_effects=True),
        name="layer",
    )(table, pictures, cotangent, kernel, analysis, synthesis)


def per_device(images, cotangent, kernel):
    total = images.shape[0] * lax.axis_size("sample") * lax.axis_size("freq")
    return layer(images, cotangent, kernel, total)


def solution(mesh):
    placed = P(("sample", "freq"), None, None, None)
    return jax.shard_map(
        per_device,
        mesh=mesh,
        in_specs=(placed, placed, P()),
        out_specs=(placed, P()),
        check_vma=False,
    )
```

```python
import functools
import math

import jax
import jax.numpy as jnp
import numpy as np
from jax import lax
from jax.experimental import pallas as pl
from jax.experimental.pallas import tpu as pltpu
from jax.sharding import PartitionSpec as P

NS_STEPS = 2
GAIN = 1.6245


def transform_tables(side, images):
    half = side // 2
    freq = np.arange(half)
    cell = np.arange(side)
    angle = 2.0 * math.pi / side * ((freq[:, None] * cell[None, :]) % side)
    real_rows = np.cos(angle)
    imag_rows = -np.sin(angle)
    imag_rows[0] = np.where(cell % 2 == 0, 1.0, -1.0)
    forward = np.stack([real_rows, imag_rows])
    weight = np.full((2, half, 1), 2.0 / side)
    weight[:, 0] = 1.0 / side
    same = np.eye(images)
    analysis = np.einsum("asw,nm->asnmw", forward, same).reshape(side * images, images * side)
    synthesis = np.einsum("asw,nm->nwasm", forward * weight, same).reshape(images * side, side * images)
    return GAIN * analysis, GAIN * synthesis


def slot_tables(side, total_images):
    half = side // 2
    angle = 2.0 * math.pi / side * np.arange(half)
    cos_a, cos_b, sine = np.cos(angle), np.cos(angle), np.sin(angle)
    cos_b[0] = -1.0
    sine[0] = 0.0
    scale = np.full(half, -2.0 * 2.0 / (total_images * side * GAIN**2))
    scale[0] *= 0.5
    return np.stack([cos_a, cos_b, sine, scale]).astype(np.float32)


def hops(ahead, ring):
    x = 2 * (ahead & 1) + ahead // ring
    return sum((0, 1, 2, 1)[part] for part in (x, ahead // 8 % 4, ahead // 2 % 4))


def layer_kernel(
    images, channels, side, group, slot_table, pictures_hbm, cotangent_hbm, taps_hbm, analysis_hbm, synthesis_hbm,
    result, kernel_grad,
    pictures, cotangent, taps, analysis, synthesis, mixes, weights, base, state, other, partner, answer, total,
    chunks, from_partner, mine, received, gathered, in_sem, core_sem, chip_send, chip_recv,
):
    half = side // 2
    pair = 2 * images
    rows = side * pair
    wide = 2 * channels
    sample, freq = lax.axis_index("sample"), lax.axis_index("freq")
    ring = lax.axis_size("freq")
    chips = lax.axis_size("sample") * ring // 2
    core = sample % 2
    chip = sample // 2 * ring + freq

    def place_of(to_chip, to_core):
        return (to_chip // ring * 2 + to_core, to_chip % ring)

    def remote(source, target, send, recv, to_chip, to_core):
        return pltpu.make_async_remote_copy(
            source, target, send, recv, device_id=place_of(to_chip, to_core), device_id_type=pl.DeviceIdType.MESH
        )

    barrier = pltpu.get_barrier_semaphore()
    far_first = sorted(range(1, chips), key=lambda ahead: -hops(ahead, ring))

    loads = [
        pltpu.make_async_copy(taps_hbm, taps, in_sem.at[0]),
        pltpu.make_async_copy(analysis_hbm, analysis, in_sem.at[1]),
        pltpu.make_async_copy(pictures_hbm, pictures, in_sem.at[2]),
        pltpu.make_async_copy(cotangent_hbm, cotangent, in_sem.at[3]),
        pltpu.make_async_copy(synthesis_hbm, synthesis, in_sem.at[4]),
    ]
    for load in loads:
        load.start()
    def greet(beside, carry):
        there = place_of(chip ^ beside, jnp.where(beside == 0, 1 - core, core))
        pl.semaphore_signal(barrier, inc=1, device_id=there, device_id_type=pl.DeviceIdType.MESH)
        return carry

    lax.fori_loop(0, chips, greet, 0, unroll=8)
    loads[0].wait()
    for row in range(3):
        across = [taps[row, col].T - taps[2 - row, 2 - col] for col in range(3)]
        mixes[row, 0] = across[1]
        mixes[row, 1] = across[2] + across[0]
        mixes[row, 2] = across[0] - across[2]
    total[...] = jnp.zeros_like(total)

    for load in loads[1:4]:
        load.wait()

    def analyse(h, carry):
        both = jnp.concatenate(
            [pictures[:, h].reshape(images * side, channels), cotangent[:, h].reshape(images * side, channels)], axis=1
        )
        spectrum = jnp.dot(analysis[...], both, preferred_element_type=jnp.float32)
        spectrum = spectrum.reshape(2, half, images, wide)
        spectrum = jnp.concatenate([spectrum[..., :channels], spectrum[..., channels:]], axis=2).astype(jnp.bfloat16)
        where = pl.ds(pl.multiple_of((h + 1) * pair, pair), pair)
        base[:, where, :channels] = spectrum[0]
        base[:, where, channels:] = spectrum[1]
        return carry

    lax.fori_loop(0, side, analyse, 0, unroll=4)
    base[:, :pair] = base[:, rows : rows + pair]
    base[:, rows + pair :] = base[:, pair : 2 * pair]

    def apply(source, weight):
        stacked = jnp.concatenate([source[2 * pair :], source[pair : rows + pair], source[:rows]], axis=1)
        return jnp.dot(stacked, weight, preferred_element_type=jnp.float32)

    powers = 2 ** (NS_STEPS + 1) - 1
    last = state if powers % 2 else other

    def weigh(lane, slot):
        cos_a, cos_b, sine = slot_table[0, slot], slot_table[1, slot], slot_table[2, slot]
        for row in range(3):
            turned = (sine * mixes[row, 2]).astype(jnp.bfloat16)
            lo, hi = row * wide, row * wide + channels
            weights[lane, lo:hi, :channels] = (mixes[row, 0] + cos_a * mixes[row, 1]).astype(jnp.bfloat16)
            weights[lane, hi : hi + channels, channels:] = (mixes[row, 0] + cos_b * mixes[row, 1]).astype(jnp.bfloat16)
            weights[lane, lo:hi, channels:] = turned
            weights[lane, hi : hi + channels, :channels] = -turned

    def power(lane, slot, step):
        source = base.at[slot] if step == 0 else (state if step % 2 else other).at[lane]
        target = (other if step % 2 else state).at[lane]
        product = apply(source, weights[lane]).reshape(side, 2, images, wide)
        start = base[slot, pair : rows + pair].astype(jnp.float32).reshape(side, 2, images, wide)
        forward = start[:, 0] - product[:, 0]
        backward = start[:, 1] + product[:, 1]
        joined = jnp.stack([forward, backward], axis=1).reshape(rows, wide).astype(jnp.bfloat16)
        target[pair : rows + pair] = joined
        if step < powers - 1:
            target[:pair] = joined[rows - pair :]
            target[rows + pair :] = joined[:pair]
        else:
            finished = (2.0 / GAIN**2) * forward - (1.0 / GAIN**2) * start[:, 0]
            answer[slot] = finished.reshape(side * images, wide)
            crossed = jnp.stack([-backward, forward], axis=1).reshape(rows, wide).astype(jnp.bfloat16)
            partner[lane, pair:] = crossed
            partner[lane, :pair] = crossed[rows - pair :]

    def correlate(lane, slot):
        cos_a, cos_b, sine, scale = (slot_table[k, slot] for k in range(4))
        left = last[lane, pair : rows + pair]
        for row, right in enumerate((partner[lane, pair:], partner[lane, :rows])):
            outer = lax.dot_general(left, right, (((0,), (0,)), ((), ())), preferred_element_type=jnp.float32)
            outer = outer * scale
            first, second = outer[:channels, :channels], outer[channels:, channels:]
            total[row, 0] += first + second
            total[row, 1] += cos_a * first + cos_b * second
            total[row, 2] += sine * (outer[channels:, :channels] - outer[:channels, channels:])

    early, late = (0, 1), (2, 3)
    for lane in early:
        weigh(lane, lane)
    for lane in late:
        last[lane] = jnp.zeros_like(last[lane])
        partner[lane] = jnp.zeros_like(partner[lane])

    def slot_group(index, carry):
        slot = [index * group + lane for lane in range(group)]
        before = [jnp.maximum(slot[lane] - group, 0) for lane in range(group)]
        after = [jnp.minimum(slot[lane] + group, half - 1) for lane in range(group)]
        for lane in early:
            power(lane, slot[lane], 0)
            correlate(lane + 2, before[lane + 2])
        for step in range(1, powers - 1):
            for lane in early:
                power(lane, slot[lane], step)
                if step == 2:
                    weigh(lane + 2, slot[lane + 2])
        for lane in early:
            power(lane + 2, slot[lane + 2], 0)
            power(lane, slot[lane], powers - 1)
        for lane in early:
            power(lane + 2, slot[lane + 2], 1)
            correlate(lane, slot[lane])
        for step in range(2, powers):
            for lane in late:
                power(lane, slot[lane], step)
                if step == 3:
                    weigh(lane - 2, after[lane - 2])
        return carry

    lax.fori_loop(0, half // group, slot_group, 0)
    for lane in late:
        correlate(lane, half - group + lane)

    def lay(place, piece):
        chunks[:, :, place] = piece.reshape(2, chips, channels)

    lay(0, total[0, 0])
    lay(1, total[0, 1] - total[0, 2])
    lay(2, total[1, 0])
    lay(3, total[1, 1] - total[1, 2])
    lay(4, total[1, 1] + total[1, 2])
    pl.semaphore_wait(barrier, chips)
    swap = remote(chunks.at[1 - core], from_partner, core_sem.at[0], core_sem.at[1], chip, 1 - core)
    swap.start()
    loads[4].wait()

    def synthesise(index, carry):
        columns = []
        for part in range(2):
            where = pl.ds(pl.multiple_of((2 * index + part) * images, images), images)
            tiles = [answer[:, where, k * channels : (k + 1) * channels].reshape(half * images, channels) for k in range(2)]
            columns.append(jnp.concatenate(tiles, axis=0).astype(jnp.bfloat16))
        maps = jnp.dot(synthesis[...], jnp.concatenate(columns, axis=1), preferred_element_type=jnp.float32)
        maps = maps.astype(jnp.bfloat16)
        for part in range(2):
            result[:, 2 * index + part] = maps[:, part * channels : (part + 1) * channels].reshape(images, side, channels)
        return carry

    third = side // 6
    lax.fori_loop(0, third, synthesise, 0, unroll=True)
    swap.wait()
    mine[...] = chunks[core] + from_partner[...]

    for ahead in far_first:
        there = chip ^ ahead
        remote(mine.at[there], received.at[ahead - 1], chip_send.at[0], chip_recv.at[0], there, core).start()
    lax.fori_loop(third, 2 * third, synthesise, 0, unroll=True)
    everything = pltpu.make_async_copy(received, received, chip_recv.at[0])
    everything.wait()
    pltpu.make_async_copy(received, received, chip_send.at[0]).wait()
    gathered[core, chip] = mine[chip] + jnp.sum(received[...], axis=0)

    piece = gathered.at[core, chip]
    for ahead in far_first:
        remote(piece, piece, chip_send.at[1], chip_recv.at[1], chip ^ ahead, core).start()
    lax.fori_loop(2 * third, side // 2, synthesise, 0, unroll=True)
    pltpu.make_async_copy(received, received, chip_recv.at[1]).wait()
    pltpu.make_async_copy(received, received, chip_send.at[1]).wait()
    ours = gathered.at[core]
    swap = remote(ours, ours, core_sem.at[2], core_sem.at[3], chip, 1 - core)
    swap.start()
    swap.wait()

    sums = [gathered[:, :, place].reshape(channels, channels) for place in range(5)]
    for place, (row, col) in enumerate(((1, 1), (1, 2), (2, 1), (2, 2), (2, 0))):
        kernel_grad[row, col] = sums[place]
        if place:
            kernel_grad[2 - row, 2 - col] = -sums[place].T


def store_kernel(maps, gradient, maps_hbm, gradient_hbm, sems):
    stores = [
        pltpu.make_async_copy(maps, maps_hbm, sems.at[0]),
        pltpu.make_async_copy(gradient, gradient_hbm, sems.at[1]),
    ]
    for store in stores:
        store.start()
    for store in stores:
        store.wait()


def store_both(maps, gradient):
    inside = pl.BlockSpec(memory_space=pltpu.VMEM)
    outside = pl.BlockSpec(memory_space=pltpu.HBM)
    return pl.pallas_call(
        store_kernel,
        out_shape=(pltpu.HBM(maps.shape, maps.dtype), pltpu.HBM(gradient.shape, gradient.dtype)),
        in_specs=[inside, inside],
        out_specs=(outside, outside),
        scratch_shapes=[pltpu.SemaphoreType.DMA((2,))],
        compiler_params=pltpu.CompilerParams(vmem_limit_bytes=16 * 1024 * 1024),
        name="store_both",
    )(maps, gradient)


def layer(pictures, cotangent, kernel, total_images, group=4):
    images, side, _, channels = pictures.shape
    half = side // 2
    pair = 2 * images
    rows = side * pair
    wide = 2 * channels
    analysis, synthesis = transform_tables(side, images)
    analysis = jnp.asarray(analysis, jnp.bfloat16)
    synthesis = jnp.asarray(synthesis, jnp.bfloat16)
    table = jnp.asarray(slot_tables(side, total_images))
    anywhere = pl.BlockSpec(memory_space=pltpu.HBM)
    chips = lax.axis_size("sample") * lax.axis_size("freq") // 2
    return pl.pallas_call(
        functools.partial(layer_kernel, images, channels, side, group),
        out_shape=(
            pltpu.VMEM(pictures.shape, jnp.bfloat16),
            pltpu.VMEM(kernel.shape, jnp.float32),
        ),
        in_specs=[pl.BlockSpec(memory_space=pltpu.SMEM)] + [anywhere] * 5,
        out_specs=(pl.BlockSpec(memory_space=pltpu.VMEM), pl.BlockSpec(memory_space=pltpu.VMEM)),
        scratch_shapes=[
            pltpu.VMEM(pictures.shape, jnp.bfloat16),
            pltpu.VMEM(pictures.shape, jnp.bfloat16),
            pltpu.VMEM(kernel.shape, jnp.float32),
            pltpu.VMEM((wide, wide), jnp.bfloat16),
            pltpu.VMEM((wide, wide), jnp.bfloat16),
            pltpu.VMEM((3, 3, channels, channels), jnp.float32),
            pltpu.VMEM((group, 3 * wide, wide), jnp.bfloat16),
            pltpu.VMEM((half, rows + 2 * pair, wide), jnp.bfloat16),
            pltpu.VMEM((group, rows + 2 * pair, wide), jnp.bfloat16),
            pltpu.VMEM((group, rows + 2 * pair, wide), jnp.bfloat16),
            pltpu.VMEM((group, rows + pair, wide), jnp.bfloat16),
            pltpu.VMEM((half, side * images, wide), jnp.float32),
            pltpu.VMEM((2, 3, channels, channels), jnp.float32),
            pltpu.VMEM((2, chips, 5, channels), jnp.float32),
            pltpu.VMEM((chips, 5, channels), jnp.float32),
            pltpu.VMEM((chips, 5, channels), jnp.float32),
            pltpu.VMEM((chips - 1, 5, channels), jnp.float32),
            pltpu.VMEM((2, chips, 5, channels), jnp.float32),
            pltpu.SemaphoreType.DMA((5,)),
            pltpu.SemaphoreType.DMA((4,)),
            pltpu.SemaphoreType.DMA((2,)),
            pltpu.SemaphoreType.DMA((2,)),
        ],
        compiler_params=pltpu.CompilerParams(vmem_limit_bytes=60 * 1024 * 1024, collective_id=0, has_side_effects=True),
        name="layer",
    )(table, pictures, cotangent, kernel, analysis, synthesis)


def per_device(images, cotangent, kernel):
    total = images.shape[0] * lax.axis_size("sample") * lax.axis_size("freq")
    return store_both(*layer(images, cotangent, kernel, total))


def solution(mesh):
    placed = P(("sample", "freq"), None, None, None)
    return jax.shard_map(
        per_device,
        mesh=mesh,
        in_specs=(placed, placed, P()),
        out_specs=(placed, P()),
        check_vma=False,
    )
```
